128 devices in a mesh: gz: 16 (over z_hi, x, core), xy: 8 (over z_lo, y).
Axes of the slice: x: 4, y: 4, z: 4 (z_hi: 2, z_lo: 2; z = z_hi * 2 + z_lo), core: 2. Of those that a mesh axis runs over, the one named last changes fastest.
Arguments:
- prior_estimate: float32 [768, 256, 128], P('gz', 'xy'), may hold values from 0.5 to 2
- views_upright: float32 [3, 768, 256, 128], P(None, 'gz', 'xy'), may hold values from 0.2 to 5
- views_turned: float32 [3, 768, 128, 256], P(None, 'gz', 'xy'), may hold values from 0.2 to 5
- kernel_depth: float32 [6, 61], replicated, may hold values from 0.005 to 1.55, as said below
- kernel_rows: float32 [6, 31], replicated, may hold values from 0.005 to 1.55, as said below
- kernel_columns: float32 [6, 31], replicated, may hold values from 0.005 to 1.55, as said below
- lateral_offsets: int32 [6], replicated, may hold values from -8 to 8, as said below
- block_views: int32 [128, 3], replicated, may hold values from 0 to 5, all different within a row
Outputs:
- estimate: float32 [768, 256, 128], P('gz', 'xy')
The draws below stay inside these ranges and needn't reach their ends.
Inputs may be any that keep to these rules, and one draw needn't show every extreme that they name: `block_views`: row r holds 3 different views and belongs to the block at position r // 8 along gz and r % 8 along xy. `lateral_offsets`: one view has offset 8 and another -8. `kernel_depth`: positive taps. `kernel_rows`: positive taps. `kernel_columns`: positive taps.
All inputs are finite; a program needn't handle non-finite values.
Results may differ from the reference program's by a relative error of at most 0.00005.
Values sent between devices are 32-bit elements; how exact they have to be, the bound alone decides.
A program may use at most 128 MiB of HBM per device.

```python
import math
import jax
import jax.numpy as jnp
from jax import lax

CZ = 48
CY = 32
VIEWS = 6
ACTIVE = 3
HZ = 61
HY = 31
HX = 31
OFF = 8
ITERS = 2
HALF = 3
NZ = 768
NY = 256
NX = 128
NBLOCKS = 128
N_GZ = 16
N_XY = 8


def draw_lateral_offsets(key, part):
    value_key = jax.random.fold_in(key, 11)
    perm_key = jax.random.fold_in(key, 23)
    values = jax.random.randint(value_key, (VIEWS,), -OFF, OFF + 1, dtype=jnp.int32)
    ranking = jax.random.permutation(perm_key, VIEWS)
    values = values.at[ranking[0]].set(OFF)
    values = values.at[ranking[1]].set(-OFF)
    return values


def tap_profile(key, extent, width_low, width_high, ripple_low, ripple_high):
    radius = (extent - 1) // 2
    width_key = jax.random.fold_in(key, 3)
    base_key = jax.random.fold_in(key, 5)
    ripple_key = jax.random.fold_in(key, 7)
    breadth = jnp.exp(jax.random.uniform(width_key, (VIEWS, 1), jnp.float32, jnp.log(width_low), jnp.log(width_high)))
    places = jnp.arange(extent, dtype=jnp.float32)[None, :] - radius
    profile = jnp.exp(-0.5 * (places / breadth) ** 2)
    baseline = jax.random.uniform(base_key, (VIEWS, 1), jnp.float32, 0.01, 0.03)
    ripple = jax.random.uniform(ripple_key, (VIEWS, extent), jnp.float32, ripple_low, ripple_high)
    return ((profile + baseline) * ripple).astype(jnp.float32)


def draw_kernel_depth(key, part):
    inner_key = jax.random.fold_in(key, 101)
    return tap_profile(inner_key, HZ, 3.0, 6.0, 0.6, 1.4)


def draw_kernel_rows(key, part):
    inner_key = jax.random.fold_in(key, 202)
    return tap_profile(inner_key, HY, 1.0, 2.0, 0.6, 1.4)


def draw_kernel_columns(key, part):
    inner_key = jax.random.fold_in(key, 303)
    return tap_profile(inner_key, HX, 1.0, 2.0, 0.6, 1.4)


def levels(rng, shape, cuts, smallest, top_value):
    def one(dim, parts):
        heights = jax.random.uniform(jax.random.fold_in(jax.random.fold_in(rng, 6), dim), (parts,), jnp.float32, smallest / len(cuts), top_value / len(cuts))
        return jnp.repeat(jnp.exp(heights), shape[dim] // parts).reshape((-1,) + (1,) * (len(shape) - dim - 1))

    loudness = one(*cuts[0])
    for cut in cuts[1:]:
        loudness = loudness * one(*cut)
    return loudness


def distinct(own_key, rows, number_of, top, lift):
    sequence = jax.random.permutation(jax.random.fold_in(own_key, 1), number_of)
    favour = sequence
    for power in range(3):
        favour = favour * favour // number_of
    favour = favour * lift // number_of
    tickets = jax.random.randint(jax.random.fold_in(own_key, 2), (rows, number_of), 0, 4096) + favour
    holders = jax.random.permutation(jax.random.fold_in(own_key, 3), rows)[jnp.arange(number_of) % rows]
    tickets = jnp.where(jnp.arange(rows)[:, None] == holders[None, :], 1 << 14, tickets)
    priority = tickets * number_of + jnp.arange(number_of)
    return lax.top_k(priority.astype(jnp.int32), top)[1].astype(jnp.int32)


def setup_inputs(seed: int = 0) -> dict:
    key_of = jax.random.split(jax.random.key(seed), 9)
    return {
        "prior_estimate": jnp.clip(jnp.exp(math.log(2.0) - 1.3862944 * jax.random.uniform(key_of[0], (NZ, NY, NX), jnp.float32) ** levels(key_of[0], (NZ, NY, NX), ((0, 16), (1, 8)), -0.2, 0.2)), 0.5, 2.0),
        "views_upright": jnp.clip(jnp.exp(math.log(5.0) - 3.218876 * jax.random.uniform(key_of[1], (HALF, NZ, NY, NX), jnp.float32) ** levels(key_of[1], (HALF, NZ, NY, NX), ((1, 16), (2, 8)), -0.2, 0.2)), 0.2, 5.0),
        "views_turned": jnp.clip(jnp.exp(math.log(5.0) - 3.218876 * jax.random.uniform(key_of[2], (HALF, NZ, NX, NY), jnp.float32) ** levels(key_of[2], (HALF, NZ, NX, NY), ((1, 16), (2, 8)), -0.2, 0.2)), 0.2, 5.0),
        "kernel_depth": draw_kernel_depth(jax.random.fold_in(key_of[8], 71), 0),
        "kernel_rows": draw_kernel_rows(jax.random.fold_in(key_of[8], 71), 0),
        "kernel_columns": draw_kernel_columns(jax.random.fold_in(key_of[8], 71), 0),
        "lateral_offsets": draw_lateral_offsets(jax.random.fold_in(key_of[8], 71), 0),
        "block_views": distinct(key_of[7], NBLOCKS, VIEWS, ACTIVE, 4096),
    }


def normalize(kernel):
    return kernel / jnp.sum(kernel, axis=-1, keepdims=True)


def axis_pass(volume, kernel, axis, reverse):
    extent = kernel.shape[0]
    radius = (extent - 1) // 2
    length = volume.shape[axis]
    padding = [(0, 0), (0, 0), (0, 0)]
    padding[axis] = (radius, radius)
    padded = jnp.pad(volume, padding)
    summed = jnp.zeros_like(volume)
    for tap_index in range(extent):
        anchor = 2 * radius - tap_index if reverse else tap_index
        summed = summed + kernel[tap_index] * lax.slice_in_dim(padded, anchor, anchor + length, axis=2 if axis == 2 else axis)
    return summed


def lateral_pass(volume, kernel, displacement, reverse):
    extent = kernel.shape[0]
    radius = (extent - 1) // 2
    margin = radius + OFF
    length = volume.shape[2]
    padded = jnp.pad(volume, ((0, 0), (0, 0), (margin, margin)))
    summed = jnp.zeros_like(volume)
    for tap_index in range(extent):
        if reverse:
            anchor = 2 * radius + OFF + displacement - tap_index
        else:
            anchor = OFF + tap_index - displacement
        window = lax.dynamic_slice_in_dim(padded, anchor.astype(jnp.int32), length, 2)
        summed = summed + kernel[tap_index] * window
    return summed


def reference(prior_estimate, views_upright, views_turned, kernel_depth, kernel_rows, kernel_columns, lateral_offsets, block_views):
    taps_depth = normalize(kernel_depth)
    taps_rows = normalize(kernel_rows)
    taps_columns = normalize(kernel_columns)
    turned = jnp.transpose(views_turned, (0, 1, 3, 2))
    observed = jnp.concatenate([views_upright, turned], axis=0)
    member = jnp.sum((block_views[:, :, None] == jnp.arange(VIEWS, dtype=jnp.int32)[None, None, :]).astype(jnp.float32), axis=1) / ACTIVE
    layout = member.reshape(N_GZ, N_XY, VIEWS)
    weight_field = jnp.repeat(jnp.repeat(layout, CZ, axis=0), CY, axis=1)
    estimate = prior_estimate
    for iteration in range(ITERS):
        correction = jnp.zeros_like(estimate)
        for view_index in range(VIEWS):
            blurred = axis_pass(estimate, taps_depth[view_index], 0, False)
            blurred = axis_pass(blurred, taps_rows[view_index], 1, False)
            blurred = lateral_pass(blurred, taps_columns[view_index], lateral_offsets[view_index], False)
            quotient = observed[view_index] / blurred
            back = axis_pass(quotient, taps_depth[view_index], 0, True)
            back = axis_pass(back, taps_rows[view_index], 1, True)
            back = lateral_pass(back, taps_columns[view_index], lateral_offsets[view_index], True)
            correction = correction + weight_field[:, :, view_index][:, :, None] * back
        estimate = estimate * correction
    return estimate
```

```python
import functools

import jax
import jax.numpy as jnp
from jax import lax
from jax.experimental import pallas as pl
from jax.experimental.pallas import tpu as pltpu
from jax.sharding import PartitionSpec as P

ITERS = 2
F32 = jnp.float32
BF16 = jnp.bfloat16
MESH = pl.DeviceIdType.MESH


def split(value):
    high = value.astype(BF16)
    low = (value - high.astype(F32)).astype(BF16)
    return high, low


def banded(taps_ref, view, index, extent):
    total = lax.fori_loop(0, extent, lambda k, s: s + taps_ref[view, k], jnp.float32(0.0))

    def one(k, mat):
        return jnp.where(index == k, taps_ref[view, k], mat)

    mat = lax.fori_loop(0, extent, one, jnp.zeros(index.shape, F32))
    return mat / jnp.full(index.shape, total, F32)


def kernel(
    nz, ny, views, halfv, n_gz, n_xy, hz, hy, hx,
    kd_ref, kr_ref, kc_ref, off_ref, bv_ref, est_hbm, up_hbm, vt_hbm,
    out_ref,
    ext, mid, cor, rz, ry, obs, vt, pack, recv,
    zl, zf, stack, zt, yf, ya, xf, xa,
    load_sem, fz_send, fz_recv, fy_send, fy_recv, fc_send, fc_recv,
    az_send, az_recv, ac_send, ac_recv, ay_send, ay_recv, t_send, t_recv,
):
    g = lax.axis_index("gz")
    r = lax.axis_index("xy")
    rz_n = (hz - 1) // 2
    top = rz_n + nz
    cols = ny // 2
    has = {"zu": g < n_gz - 1, "zd": g > 0, "yu": r < n_xy - 1, "yd": r > 0}
    opposite = {"zu": "zd", "zd": "zu", "yu": "yd", "yd": "yu"}
    target = {"zu": {"gz": g + 1}, "zd": {"gz": g - 1}, "yu": {"xy": r + 1}, "yd": {"xy": r - 1}}

    loads = [
        pltpu.make_async_copy(est_hbm, ext.at[pl.ds(rz_n, nz), pl.ds(16, ny), :], load_sem.at[0]),
        pltpu.make_async_copy(vt_hbm, vt, load_sem.at[1]),
        pltpu.make_async_copy(up_hbm, obs.at[pl.ds(0, halfv)], load_sem.at[2]),
    ]
    for load in loads:
        load.start()

    barrier = pltpu.get_barrier_semaphore()
    for d in range(1, n_xy):
        pl.semaphore_signal(
            barrier, inc=1, device_id={"xy": lax.rem(r + d, n_xy)}, device_id_type=MESH
        )
    for way in ("zu", "zd"):
        @pl.when(has[way])
        def _():
            pl.semaphore_signal(barrier, inc=1, device_id=target[way], device_id_type=MESH)

    ext[pl.ds(top + rz_n, ext.shape[0] - top - rz_n)] = jnp.zeros(
        (ext.shape[0] - top - rz_n,) + ext.shape[1:], F32
    )

    @pl.when(jnp.logical_not(has["zd"]))
    def _():
        @pl.loop(0, rz_n)
        def _(i):
            ext[i] = jnp.zeros(ext.shape[1:], F32)

    @pl.when(jnp.logical_not(has["zu"]))
    def _():
        @pl.loop(top, top + rz_n)
        def _(i):
            ext[i] = jnp.zeros(ext.shape[1:], F32)

    @pl.when(jnp.logical_not(has["yd"]))
    def _():
        @pl.loop(rz_n, top)
        def _(i):
            ext[i, pl.ds(0, 16), :] = jnp.zeros((16, 128), F32)

    @pl.when(jnp.logical_not(has["yu"]))
    def _():
        @pl.loop(rz_n, top)
        def _(i):
            ext[i, pl.ds(16 + ny, 16), :] = jnp.zeros((16, 128), F32)

    def flow(way, src, dst, send, recv_sem, number):
        def make():
            return pltpu.make_async_remote_copy(
                src_ref=src, dst_ref=dst, send_sem=send.at[number], recv_sem=recv_sem.at[number],
                device_id=target[way], device_id_type=MESH,
            )

        def start():
            @pl.when(has[way])
            def _():
                make().start()

        def arrived():
            @pl.when(has[opposite[way]])
            def _():
                make().wait_recv()

        def sent():
            @pl.when(has[way])
            def _():
                make().wait_send()

        return start, arrived, sent

    def cut(ref, z0, count, y0, width):
        return ref.at[pl.ds(z0, count), pl.ds(y0, width), :]

    low_src, high_src = rz_n, top - rz_n
    fz = [
        flow("zu", cut(ext, high_src, rz_n, 16, ny), cut(ext, 0, rz_n, 16, ny), fz_send, fz_recv, 0),
        flow("zd", cut(ext, low_src, rz_n, 16, ny), cut(ext, top, rz_n, 16, ny), fz_send, fz_recv, 1),
    ]
    fy = [
        flow("yu", cut(ext, rz_n, nz, ny, 16), cut(ext, rz_n, nz, 0, 16), fy_send, fy_recv, 0),
        flow("yd", cut(ext, rz_n, nz, 16, 16), cut(ext, rz_n, nz, 16 + ny, 16), fy_send, fy_recv, 1),
    ]
    fc = []
    for n, y0 in enumerate((0, 16 + ny)):
        fc.append(flow("zu", cut(ext, high_src, rz_n, y0, 16), cut(ext, 0, rz_n, y0, 16), fc_send, fc_recv, 2 * n))
        fc.append(flow("zd", cut(ext, low_src, rz_n, y0, 16), cut(ext, top, rz_n, y0, 16), fc_send, fc_recv, 2 * n + 1))
    ac = []
    for n, y0 in enumerate((0, 16 + ny)):
        ac.append(flow("zu", cut(cor, top, rz_n, y0, 16), cut(rz.at[0], 0, rz_n, y0, 16), ac_send, ac_recv, 2 * n))
        ac.append(flow("zd", cut(cor, 0, rz_n, y0, 16), cut(rz.at[1], 0, rz_n, y0, 16), ac_send, ac_recv, 2 * n + 1))
    az = [
        flow("zu", cut(cor, top, rz_n, 16, ny), cut(rz.at[0], 0, rz_n, 16, ny), az_send, az_recv, 0),
        flow("zd", cut(cor, 0, rz_n, 16, ny), cut(rz.at[1], 0, rz_n, 16, ny), az_send, az_recv, 1),
    ]
    ay = [
        flow("yu", cut(cor, rz_n, nz, 16 + ny, 16), ry.at[0], ay_send, ay_recv, 0),
        flow("yd", cut(cor, rz_n, nz, 0, 16), ry.at[1], ay_send, ay_recv, 1),
    ]

    def begin(flows):
        for f in flows:
            f[0]()

    def await_all(flows):
        for f in flows:
            f[1]()

    def drain(flows):
        for f in flows:
            f[2]()

    loads[0].wait()
    greeted = n_xy - 1 + has["zu"].astype(jnp.int32) + has["zd"].astype(jnp.int32)
    pl.semaphore_wait(barrier, greeted)
    begin(fy)
    begin(fz)

    loads[1].wait()
    octets = nz // 8

    @pl.loop(0, halfv * octets)
    def _(i):
        view = i // octets
        octet = i % octets
        block = vt[view, pl.ds(octet * 8, 8)].reshape(128, ny * n_xy)
        for half in range(2):
            part = block[:, half * 128:(half + 1) * 128].T
            for piece in range(128 // ny):
                pack[half * (128 // ny) + piece, i] = part[piece * ny:(piece + 1) * ny]

    def turn(d):
        peer = lax.rem(r + d, n_xy)
        return pltpu.make_async_remote_copy(
            src_ref=pack.at[peer], dst_ref=recv.at[r], send_sem=t_send.at[d - 1], recv_sem=t_recv.at[d - 1],
            device_id={"xy": peer}, device_id_type=MESH,
        )

    for d in range(1, n_xy):
        turn(d).start()

    @pl.loop(0, halfv * octets)
    def _(i):
        recv[r, i] = pack[r, i]

    row = lambda shape: lax.broadcasted_iota(jnp.int32, shape, 0)
    lane = lambda shape: lax.broadcasted_iota(jnp.int32, shape, 1)

    @pl.loop(0, views)
    def _(v):
        s = (nz, 128)
        depth = banded(kd_ref, v, lane(s) - row(s), hz)
        zf[pl.ds(v * nz, nz), :] = depth
        high, low = split(depth)
        zl[pl.ds(v * nz, nz), 0:128] = high
        zl[pl.ds(v * nz, nz), 128:256] = high
        zl[pl.ds(v * nz, nz), 256:384] = low
        s = (ny, 256)
        rows = banded(kr_ref, v, (lane(s) & 63) - 1 - row(s), hy)
        high, low = split(rows)
        yf[v] = jnp.where(lane(s) < 128, high.astype(F32), low.astype(F32)).astype(BF16)
        s = (64, 128)
        rows = banded(kr_ref, v, row(s) - 1 - (lane(s) & 31), hy)
        high, low = split(rows)
        ya[v] = jnp.where(lane(s) < 64, high.astype(F32), low.astype(F32)).astype(BF16)
        s = (128, 128)
        shift = (hx - 1) // 2 + off_ref[0, v]
        for ref, sign in ((xf, 1), (xa, -1)):
            columns = banded(kc_ref, v, sign * (row(s) - lane(s)) + shift, hx)
            high, low = split(columns)
            ref[v, 0:128, 0:128] = high
            ref[v, 128:256, 0:128] = high
            ref[v, 0:128, 128:256] = low
            ref[v, 128:256, 128:256] = low

    kk = views * nz
    stack[...] = jnp.zeros_like(stack)
    for yb in range(3):
        @pl.loop(0, views)
        def _(v):
            s = (nz, 128)
            weights = []
            for zb in range(3):
                block = jnp.clip(g + zb - 1, 0, n_gz - 1) * n_xy + jnp.clip(r + yb - 1, 0, n_xy - 1)
                count = jnp.float32(0.0)
                for k in range(3):
                    count = count + jnp.where(bv_ref[block, k] == v, 1.0, 0.0)
                weights.append(count / 3.0)
            field = jnp.where(
                lane(s) < rz_n, weights[0], jnp.where(lane(s) < top, weights[1], weights[2])
            )
            scaled = zf[pl.ds(v * nz, nz), :] * field
            high, low = split(scaled)
            stack[pl.ds(v * nz, nz), :] = high.astype(F32)
            stack[pl.ds(kk + v * nz, nz), :] = high.astype(F32)
            stack[pl.ds(2 * kk + v * nz, nz), :] = low.astype(F32)

        for part in range(stack.shape[0] // 128):
            piece = stack[part * 128:(part + 1) * 128, :].T
            zt[yb, :, part * 128:(part + 1) * 128] = piece[0:112].astype(BF16)


    def depth_forward(y0):
        pair = jnp.concatenate(
            [ext[:, y0 + n, :] for n in range(2)], axis=1
        )
        high, low = split(pair)
        gap = jnp.zeros((16, 256), BF16)
        first = jnp.concatenate([high, gap, low, gap], axis=0)
        second = jnp.concatenate([high, gap], axis=0)
        result = jnp.dot(zl[:, 0:256], first, preferred_element_type=F32)
        result = result + jnp.dot(zl[:, 256:384], second, preferred_element_type=F32)
        for n in range(2):
            mid[:, y0 + n, :] = result[:, n * 128:(n + 1) * 128]

    def depth_adjoint(y0, yb):
        pair = jnp.concatenate(
            [mid[:, y0 + n, :] for n in range(2)], axis=1
        )
        high, low = split(pair)
        gap = jnp.zeros((stack.shape[0] - 3 * kk, 256), BF16)
        operand = jnp.concatenate([high, low, high, gap], axis=0)
        result = jnp.dot(zt[yb], operand, preferred_element_type=F32)
        for n in range(2):
            cor[:, y0 + n, :] = result[:, n * 128:(n + 1) * 128]

    group = 16

    def middle(v, z0):
        planes = []
        for p in range(group // 2):
            base = v * nz + z0 + 2 * p
            pair = jnp.concatenate([mid[base], mid[base + 1]], axis=1)
            high, low = split(pair)
            result = jnp.dot(
                yf[v, :, 0:192], jnp.concatenate([high, low, high], axis=0), preferred_element_type=F32
            )
            planes += [result[:, 0:128], result[:, 128:256]]
        data = jnp.concatenate(planes, axis=0)
        both = jnp.dot(jnp.concatenate(split(data), axis=1), xf[v], preferred_element_type=F32)
        blurred = both[:, 0:128] + both[:, 128:256]
        quotient = obs[v, pl.ds(z0, group)].reshape(group * ny, 128) / blurred
        both = jnp.dot(jnp.concatenate(split(quotient), axis=1), xa[v], preferred_element_type=F32)
        back = both[:, 0:128] + both[:, 128:256]
        for p in range(group // 2):
            base = v * nz + z0 + 2 * p
            pair = jnp.concatenate(
                [back[(2 * p) * ny:(2 * p + 1) * ny], back[(2 * p + 1) * ny:(2 * p + 2) * ny]], axis=1
            )
            high, low = split(pair)
            result = jnp.dot(
                ya[v, :, 0:96], jnp.concatenate([high, low, high], axis=0), preferred_element_type=F32
            )
            mid[base] = result[:, 0:128]
            mid[base + 1] = result[:, 128:256]

    groups = nz // group

    @pl.loop(0, ITERS)
    def _(step):
        @pl.when(step > 0)
        def _():
            begin(fy)
            begin(fz)

        await_all(fy)
        begin(fc)
        await_all(fz)

        @pl.loop(0, cols)
        def _(p):
            depth_forward(16 + 2 * p)

        await_all(fc)

        @pl.loop(0, 8)
        def _(p):
            depth_forward(2 * p)
            depth_forward(16 + ny + 2 * p)

        drain(fy)
        drain(fz)
        drain(fc)

        @pl.when(step == 0)
        def _():
            loads[2].wait()

        @pl.loop(0, halfv * groups)
        def _(i):
            middle(i // groups, (i % groups) * group)

        @pl.when(step == 0)
        def _():
            for d in range(1, n_xy):
                turn(d).wait()
            per = 128 // n_xy

            @pl.loop(0, halfv * octets)
            def _(i):
                parts = [recv[j, i] for j in range(n_xy)]
                place = lane((ny, 128)) // per
                for d in (4, 2, 1):
                    upper = (place & d) != 0
                    for a in range(n_xy):
                        if a & d:
                            continue
                        first, second = parts[a], parts[a + d]
                        parts[a] = jnp.where(upper, pltpu.roll(second, per * d, 1), first)
                        parts[a + d] = jnp.where(upper, second, pltpu.roll(first, 128 - per * d, 1))
                for j in range(n_xy):
                    obs[halfv + i // octets, (i % octets) * 8 + j] = parts[j]

        @pl.loop(0, (views - halfv) * groups)
        def _(i):
            middle(halfv + i // groups, (i % groups) * group)

        @pl.loop(0, 8)
        def _(p):
            depth_adjoint(2 * p, 0)
            depth_adjoint(16 + ny + 2 * p, 2)

        begin(ac)

        @pl.loop(0, cols)
        def _(p):
            depth_adjoint(16 + 2 * p, 1)

        begin(az)
        await_all(ac)

        def add_depth(y0, width):
            for n, z0, way in ((0, rz_n, "zd"), (1, top - rz_n, "zu")):
                @pl.when(has[way])
                def _():
                    @pl.loop(0, rz_n)
                    def _(i):
                        at = pl.ds(y0, width)
                        cor[z0 + i, at, :] = cor[z0 + i, at, :] + rz[n, i, at, :]

        add_depth(0, 16)
        add_depth(16 + ny, 16)
        begin(ay)
        await_all(az)
        add_depth(16, ny)
        await_all(ay)
        for n, y0, way in ((0, 16, "yd"), (1, ny, "yu")):
            @pl.when(has[way])
            def _():
                @pl.loop(0, nz)
                def _(i):
                    at = pl.ds(y0, 16)
                    cor[rz_n + i, at, :] = cor[rz_n + i, at, :] + ry[n, i]

        @pl.loop(0, nz)
        def _(i):
            at = pl.ds(16, ny)
            fresh = ext[rz_n + i, at, :] * cor[rz_n + i, at, :]
            ext[rz_n + i, at, :] = fresh
            out_ref[i] = fresh

        drain(ac)
        drain(az)
        drain(ay)


def solution(mesh):
    n_gz, n_xy = mesh.shape["gz"], mesh.shape["xy"]

    def local(est, upright, turned, kd, kr, kc, offsets, block_views):
        nz, ny, nx = est.shape
        views, hz = kd.shape
        hy, hx = kr.shape[1], kc.shape[1]
        halfv = upright.shape[0]
        kk = views * nz
        stacked = -(-3 * kk // 128) * 128
        dma = pltpu.SemaphoreType.DMA
        vmem = pltpu.VMEM
        smem = pl.BlockSpec(memory_space=pltpu.SMEM)
        anyspace = pl.BlockSpec(memory_space=pl.ANY)
        octets = halfv * (nz // 8)
        rz_n = (hz - 1) // 2
        return pl.pallas_call(
            functools.partial(kernel, nz, ny, views, halfv, n_gz, n_xy, hz, hy, hx),
            out_shape=jax.ShapeDtypeStruct((nz, ny, nx), F32),
            in_specs=[smem] * 5 + [anyspace] * 3,
            out_specs=pl.BlockSpec(memory_space=pltpu.VMEM),
            scratch_shapes=[
                vmem((112, 64, 128), F32),
                vmem((kk, 64, 128), F32),
                vmem((112, 64, 128), F32),
                vmem((2, rz_n, 64, 128), F32),
                vmem((2, nz, 16, 128), F32),
                vmem((views, nz, ny, 128), F32),
                vmem(turned.shape, F32),
                vmem((n_xy, octets, ny, 128), F32),
                vmem((n_xy, octets, ny, 128), F32),
                vmem((kk, 384), BF16),
                vmem((kk, 128), F32),
                vmem((stacked, 128), F32),
                vmem((3, 112, stacked), BF16),
                vmem((views, ny, 256), BF16),
                vmem((views, 64, 128), BF16),
                vmem((views, 256, 256), BF16),
                vmem((views, 256, 256), BF16),
                dma((3,)),
                dma((2,)), dma((2,)), dma((2,)), dma((2,)), dma((4,)), dma((4,)),
                dma((2,)), dma((2,)), dma((4,)), dma((4,)), dma((2,)), dma((2,)),
                dma((n_xy - 1,)), dma((n_xy - 1,)),
            ],
            compiler_params=pltpu.CompilerParams(
                collective_id=0, has_side_effects=True, vmem_limit_bytes=60 * 1024 * 1024
            ),
            name="deconvolve",
        )(kd, kr, kc, offsets.reshape(1, views), block_views, est, upright, turned)

    in_specs = (
        P("gz", "xy", None),
        P(None, "gz", "xy", None),
        P(None, "gz", "xy", None),
        P(), P(), P(), P(), P(),
    )
    return jax.shard_map(
        local, mesh=mesh, in_specs=in_specs, out_specs=P("gz", "xy", None), check_vma=False
    )
```

```python
import functools

import jax
import jax.numpy as jnp
from jax import lax
from jax.experimental import pallas as pl
from jax.experimental.pallas import tpu as pltpu
from jax.sharding import PartitionSpec as P

ITERS = 2
PITCH = 66
F32 = jnp.float32
BF16 = jnp.bfloat16
MESH = pl.DeviceIdType.MESH


def split(value):
    high = value.astype(BF16)
    low = (value - high.astype(F32)).astype(BF16)
    return high, low


def row(shape):
    return lax.broadcasted_iota(jnp.int32, shape, 0)


def lane(shape):
    return lax.broadcasted_iota(jnp.int32, shape, 1)


def kernel(
    nz, ny, views, halfv, n_gz, n_xy, hz, hy, hx,
    off_ref, kd_ref, kr_ref, kc_ref, bv_ref, est_hbm, up_hbm, vt_hbm,
    out_ref,
    ext, rim, wide, mid, cor, sc, sz, sy, rc, rz, ry, obs, vt, pack, recv,
    taps, stack, flat, zl, zt, yf, ya, xf, xa, ahead, ratio, behind,
    load_sem, fz_send, fz_recv, fy_send, fy_recv, fc_send, fc_recv,
    az_send, az_recv, ac_send, ac_recv, ay_send, ay_recv, t_send, t_recv,
):
    g = lax.axis_index("gz")
    r = lax.axis_index("xy")
    rz_n = (hz - 1) // 2
    top = rz_n + nz
    kk = views * nz
    only = nz - rz_n
    spans = ((only, rz_n), (0, only), (rz_n, nz))
    has = {"zu": g < n_gz - 1, "zd": g > 0, "yu": r < n_xy - 1, "yd": r > 0}
    opposite = {"zu": "zd", "zd": "zu", "yu": "yd", "yd": "yu"}
    target = {"zu": {"gz": g + 1}, "zd": {"gz": g - 1}, "yu": {"xy": r + 1}, "yd": {"xy": r - 1}}

    loads = [
        pltpu.make_async_copy(est_hbm, ext.at[pl.ds(rz_n, nz)], load_sem.at[0]),
        pltpu.make_async_copy(vt_hbm, vt, load_sem.at[1]),
        pltpu.make_async_copy(up_hbm, obs.at[pl.ds(0, halfv)], load_sem.at[2]),
    ]
    for load in loads:
        load.start()

    barrier = pltpu.get_barrier_semaphore()
    for d in range(1, n_xy):
        pl.semaphore_signal(
            barrier, inc=1, device_id={"xy": lax.rem(r + d, n_xy)}, device_id_type=MESH
        )
    for way in ("zu", "zd"):
        @pl.when(has[way])
        def _():
            pl.semaphore_signal(barrier, inc=1, device_id=target[way], device_id_type=MESH)

    def clear(z0, z1, y0, y1, refs):
        @pl.loop(z0, z1)
        def _(i):
            for ref in refs:
                ref[i, pl.ds(y0, y1 - y0), :] = jnp.zeros((y1 - y0, 128), F32)

    clear(top + rz_n, ext.shape[0], 0, ny, (ext, rim))

    @pl.when(jnp.logical_not(has["zd"]))
    def _():
        clear(0, rz_n, 0, ny, (ext, rim))

    @pl.when(jnp.logical_not(has["zu"]))
    def _():
        clear(top, top + rz_n, 0, ny, (ext, rim))

    @pl.when(jnp.logical_not(has["yd"]))
    def _():
        clear(rz_n, top, 0, 16, (rim,))

    @pl.when(jnp.logical_not(has["yu"]))
    def _():
        clear(rz_n, top, 16, 32, (rim,))

    def flow(way, src, dst, send, recv_sem, number):
        def make():
            return pltpu.make_async_remote_copy(
                src_ref=src, dst_ref=dst, send_sem=send.at[number], recv_sem=recv_sem.at[number],
                device_id=target[way], device_id_type=MESH,
            )

        def start():
            @pl.when(has[way])
            def _():
                make().start()

        def arrived():
            @pl.when(has[opposite[way]])
            def _():
                make().wait_recv()

        def sent():
            @pl.when(has[way])
            def _():
                make().wait_send()

        return start, arrived, sent

    def rows(ref, z0, z1):
        return ref.at[pl.ds(z0, z1 - z0)]

    def cut(ref, z0, z1, y0):
        return ref.at[pl.ds(z0, z1 - z0), pl.ds(y0, 16), :]

    fz = [
        flow("zu", rows(ext, top - rz_n, top), rows(ext, 0, rz_n), fz_send, fz_recv, 0),
        flow("zd", rows(ext, rz_n, 2 * rz_n), rows(ext, top, top + rz_n), fz_send, fz_recv, 1),
    ]
    fy = []
    for n, (a, b) in enumerate(spans):
        a, b = rz_n + a, rz_n + b
        fy.append([
            flow("yu", cut(ext, a, b, ny - 16), cut(rim, a, b, 0), fy_send, fy_recv, 2 * n),
            flow("yd", cut(ext, a, b, 0), cut(rim, a, b, 16), fy_send, fy_recv, 2 * n + 1),
        ])
    fc = [
        [
            flow("zu", rows(rim, rz_n + only, 2 * rz_n), rows(rim, 0, rz_n - only), fc_send, fc_recv, 0),
            flow("zd", rows(rim, rz_n + only, 2 * rz_n), rows(rim, top + only, top + rz_n), fc_send, fc_recv, 1),
        ],
        [flow("zd", rows(rim, rz_n, rz_n + only), rows(rim, top, top + only), fc_send, fc_recv, 2)],
        [flow("zu", rows(rim, 2 * rz_n, top), rows(rim, rz_n - only, rz_n), fc_send, fc_recv, 3)],
    ]
    ac = [
        [flow("zu", rows(sc.at[0], 0, only), rows(rc.at[0], 0, only), ac_send, ac_recv, 0)],
        [flow("zd", rows(sc.at[1], rz_n - only, rz_n), rows(rc.at[1], rz_n - only, rz_n), ac_send, ac_recv, 1)],
        [
            flow("zu", rows(sc.at[0], only, rz_n), rows(rc.at[0], only, rz_n), ac_send, ac_recv, 2),
            flow("zd", rows(sc.at[1], 0, rz_n - only), rows(rc.at[1], 0, rz_n - only), ac_send, ac_recv, 3),
        ],
    ]
    az = [
        flow("zu", sz.at[0], rz.at[0], az_send, az_recv, 0),
        flow("zd", sz.at[1], rz.at[1], az_send, az_recv, 1),
    ]
    ay = []
    for n, (a, b) in enumerate((spans[1], spans[2], spans[0])):
        ay.append([
            flow("yu", rows(sy.at[0], a, b), rows(ry.at[0], a, b), ay_send, ay_recv, 2 * n),
            flow("yd", rows(sy.at[1], a, b), rows(ry.at[1], a, b), ay_send, ay_recv, 2 * n + 1),
        ])

    def begin(flows):
        for f in flows:
            f[0]()

    def await_all(flows):
        for f in flows:
            f[1]()

    def drain(flows):
        for f in flows:
            f[2]()

    loads[0].wait()
    greeted = n_xy - 1 + has["zu"].astype(jnp.int32) + has["zd"].astype(jnp.int32)
    pl.semaphore_wait(barrier, greeted)
    for part in fy:
        begin(part)
    begin(fz)

    loads[1].wait()
    octets = nz // 8

    @pl.loop(0, halfv * octets)
    def _(i):
        block = vt[i // octets, pl.ds((i % octets) * 8, 8)].reshape(128, ny * n_xy)
        for half in range(2):
            part = block[:, half * 128:(half + 1) * 128].T
            for piece in range(128 // ny):
                pack[half * (128 // ny) + piece, i] = part[piece * ny:(piece + 1) * ny]

    def turn(d):
        peer = lax.rem(r + d, n_xy)
        return pltpu.make_async_remote_copy(
            src_ref=pack.at[peer], dst_ref=recv.at[r], send_sem=t_send.at[d - 1], recv_sem=t_recv.at[d - 1],
            device_id={"xy": peer}, device_id_type=MESH,
        )

    for d in range(1, n_xy):
        turn(d).start()

    @pl.loop(0, halfv * octets)
    def _(i):
        recv[r, i] = pack[r, i]

    taps[...] = jnp.zeros_like(taps)
    for n, ref in enumerate((kd_ref, kr_ref, kc_ref)):
        value = ref[...]
        value = value / jnp.sum(value, axis=1, keepdims=True)
        taps[n, 0:views, 0:value.shape[1]] = value
        if n == 1:
            taps[n, 0:views, 64:64 + value.shape[1]] = value
    stack[...] = jnp.zeros_like(stack)

    @pl.loop(0, views)
    def _(v):
        def toeplitz(line, count, shift):
            return pltpu.roll(jnp.broadcast_to(line, (count, 128)), shift, 1, stride=1, stride_axis=0)

        depth = toeplitz(taps[0, pl.ds(v, 1), :], nz, 0)
        for n in range(3):
            stack[pl.ds(n * kk + v * nz, nz), :] = depth
        high, low = split(depth)
        zl[pl.ds(v * nz, nz), 0:128] = high
        zl[pl.ds(v * nz, nz), 128:256] = high
        zl[pl.ds(v * nz, nz), 256:384] = low

        line = toeplitz(taps[1, pl.ds(v, 1), :], ny, 1)
        high, low = split(line)
        yf[v, :, 0:128] = high
        yf[v, :, 128:256] = low
        line = jnp.concatenate([line] * (128 // ny), axis=0).T[0:64]
        high, low = split(line)
        ya[v] = jnp.where(lane((64, 128)) < 64, high.astype(F32), low.astype(F32)).astype(BF16)

        s = (128, 128)
        reach = (hx - 1) // 2
        shift = off_ref[0, v] + reach
        tap = lane(s) - row(s) + shift
        line = pltpu.roll(jnp.broadcast_to(taps[2, pl.ds(v, 1), :], (8, 128)), 128 - shift, 1)[0:1]
        column = jnp.where((tap >= 0) & (tap < hx), toeplitz(line, 128, 0), 0.0)
        for ref, matrix in ((xa, column), (xf, column.T)):
            high, low = split(matrix)
            ref[v, 0:128, 0:128] = high
            ref[v, 128:256, 0:128] = high
            ref[v, 0:128, 128:256] = low
            ref[v, 128:256, 128:256] = low

    for part in range(stack.shape[0] // 128):
        flat[:, part * 128:(part + 1) * 128] = stack[part * 128:(part + 1) * 128, :].T[0:112]

    for yb in range(3):
        fields = []
        for zb in range(3):
            block = jnp.clip(g + zb - 1, 0, n_gz - 1) * n_xy + jnp.clip(r + yb - 1, 0, n_xy - 1)
            chosen = bv_ref[pl.ds(block, 1), :]
            view = lax.rem(lane((1, stack.shape[0])), kk) // nz
            field = jnp.zeros((1, stack.shape[0]), F32)
            for k in range(bv_ref.shape[1]):
                one = jnp.broadcast_to(chosen[:, k:k + 1], (1, stack.shape[0]))
                field = field + jnp.where(one == view, 1.0, 0.0)
            fields.append(field / float(bv_ref.shape[1]))

        for i in range(7):
            s = (16, stack.shape[0])
            number = row(s) + 16 * i
            field = jnp.where(number < rz_n, fields[0], jnp.where(number < top, fields[1], fields[2]))
            scaled = flat[16 * i:16 * i + 16, :] * field
            high, low = split(scaled)
            high, low = high.astype(F32), low.astype(F32)
            chosen = jnp.where(lane(s) < 2 * kk, high, low)
            zt[yb, 16 * i:16 * i + 16, :] = chosen.astype(BF16)

    def widen(source, z0, z1, y0, width, to):
        @pl.loop(z0, z1)
        def _(i):
            wide[pl.ds(i * PITCH + to, width), :] = source[i, pl.ds(y0, width), :]

    def widen_rim(z0, z1):
        widen(rim, z0, z1, 0, 16, 0)
        widen(rim, z0, z1, 16, 16, 16 + ny)

    def depth_forward(y0):
        pair = jnp.concatenate(
            [wide[pl.ds(y0 + n, 112, stride=PITCH), :] for n in range(2)], axis=1
        )
        high, low = split(pair)
        gap = jnp.zeros((16, 256), BF16)
        first = jnp.concatenate([high, gap, low, gap], axis=0)
        second = jnp.concatenate([high, gap], axis=0)
        result = jnp.dot(zl[:, 0:256], first, preferred_element_type=F32)
        result = result + jnp.dot(zl[:, 256:384], second, preferred_element_type=F32)
        for n in range(2):
            mid[pl.ds(y0 + n, kk, stride=PITCH), :] = result[:, n * 128:(n + 1) * 128]

    def depth_adjoint(y0, yb):
        pair = jnp.concatenate(
            [mid[pl.ds(y0 + n, kk, stride=PITCH), :] for n in range(2)], axis=1
        )
        high, low = split(pair)
        gap = jnp.zeros((stack.shape[0] - 3 * kk, 256), BF16)
        operand = jnp.concatenate([high, low, high, gap], axis=0)
        result = jnp.dot(zt[yb], operand, preferred_element_type=F32)
        for n in range(2):
            cor[pl.ds(y0 + n, 112, stride=PITCH), :] = result[:, n * 128:(n + 1) * 128]

    group = 16
    groups = nz // group

    def middle(step):
        spare = views * nz
        count = views * groups

        @pl.loop(0, count + 3)
        def _(i):
            @pl.when((step == 0) & (i == halfv * groups))
            def _():
                unpack()

            def at(stage):
                number = jnp.clip(i - stage, 0, count - 1)
                return number // groups, (number % groups) * group

            v, z0 = at(3)
            base = jnp.where(i < 3, spare, v * nz + z0) * PITCH
            for p in range(group // 2):
                operand = jnp.concatenate([behind[p], behind[p, 0:ny]], axis=0)
                result = jnp.dot(ya[v, :, 0:96], operand, preferred_element_type=F32)
                mid[pl.ds(base + 2 * p * PITCH, 64), :] = result[:, 0:128]
                mid[pl.ds(base + (2 * p + 1) * PITCH, 64), :] = result[:, 128:256]

            v, z0 = at(2)
            both = jnp.dot(ratio[...], xa[v], preferred_element_type=F32)
            back = both[:, 0:128] + both[:, 128:256]
            for p in range(group // 2):
                pair = jnp.concatenate(
                    [back[(2 * p) * ny:(2 * p + 1) * ny], back[(2 * p + 1) * ny:(2 * p + 2) * ny]], axis=1
                )
                behind[p] = jnp.concatenate(split(pair), axis=0)

            v, z0 = at(1)
            both = jnp.dot(ahead[...], xf[v], preferred_element_type=F32)
            blurred = both[:, 0:128] + both[:, 128:256]
            quotient = obs[v, pl.ds(z0, group)].reshape(group * ny, 128) / blurred
            ratio[...] = jnp.concatenate(split(quotient), axis=1)

            v, z0 = at(0)
            base = (v * nz + z0) * PITCH
            for p in range(group // 2):
                pair = jnp.concatenate(
                    [mid[pl.ds(base + (2 * p + n) * PITCH, 64), :] for n in range(2)], axis=1
                )
                high, low = split(pair)
                result = jnp.dot(
                    yf[v, :, 0:192], jnp.concatenate([high, low, high], axis=0), preferred_element_type=F32
                )
                for n in range(2):
                    ahead[(2 * p + n) * ny:(2 * p + n + 1) * ny, :] = jnp.concatenate(
                        split(result[:, n * 128:(n + 1) * 128]), axis=1
                    )

    def unpack():
        for d in range(1, n_xy):
            turn(d).wait()
        per = 128 // n_xy

        @pl.loop(0, halfv * octets)
        def _(i):
            parts = [recv[j, i] for j in range(n_xy)]
            place = lane((ny, 128)) // per
            for d in (4, 2, 1):
                upper = (place & d) != 0
                for a in range(n_xy):
                    if a & d:
                        continue
                    first, second = parts[a], parts[a + d]
                    parts[a] = jnp.where(upper, pltpu.roll(second, per * d, 1), first)
                    parts[a + d] = jnp.where(upper, second, pltpu.roll(first, 128 - per * d, 1))
            for j in range(n_xy):
                obs[halfv + i // octets, (i % octets) * 8 + j] = parts[j]

    def add_depth(source, n, z0, i0, i1, pieces, way):
        @pl.when(has[way])
        def _():
            @pl.loop(i0, i1)
            def _(i):
                for y0, width, to in pieces:
                    at = pl.ds((rz_n + z0 + i) * PITCH + to, width)
                    cor[at, :] = cor[at, :] + source[n, i, pl.ds(y0, width), :]

    sides = ((0, 16, 0), (16, 16, 16 + ny))
    whole = ((0, ny, 16),)

    def give(n):
        a, b = (spans[1], spans[2], spans[0])[n]

        @pl.loop(a, b)
        def _(i):
            sy[0, i] = cor[pl.ds((rz_n + i) * PITCH + 16 + ny, 16), :]
            sy[1, i] = cor[pl.ds((rz_n + i) * PITCH, 16), :]

        begin(ay[n])

    @pl.loop(0, ITERS)
    def _(step):
        @pl.when(step > 0)
        def _():
            for part in fy:
                begin(part)
            begin(fz)

        widen(ext, rz_n, top, 0, ny, 16)
        for n in range(3):
            await_all(fy[n])
            begin(fc[n])
        widen_rim(rz_n, top)
        await_all(fz)
        widen(ext, 0, rz_n, 0, ny, 16)
        widen(ext, top, ext.shape[0], 0, ny, 16)

        @pl.loop(0, ny // 4)
        def _(p):
            depth_forward(16 + 4 * p)
            depth_forward(18 + 4 * p)

        for n in range(3):
            await_all(fc[n])
        widen_rim(0, rz_n)
        widen_rim(top, ext.shape[0])

        @pl.loop(0, 8)
        def _(p):
            depth_forward(2 * p)
            depth_forward(16 + ny + 2 * p)

        for n in range(3):
            drain(fy[n])
            drain(fc[n])
        drain(fz)

        @pl.when(step == 0)
        def _():
            loads[2].wait()

        middle(step)

        @pl.loop(0, 8)
        def _(p):
            depth_adjoint(2 * p, 0)
            depth_adjoint(16 + ny + 2 * p, 2)

        def pick(dest, y0, width, to):
            @pl.loop(0, rz_n)
            def _(i):
                dest[0, i, pl.ds(to, width), :] = cor[pl.ds((top + i) * PITCH + y0, width), :]
                dest[1, i, pl.ds(to, width), :] = cor[pl.ds(i * PITCH + y0, width), :]

        pick(sc, 0, 16, 0)
        pick(sc, 16 + ny, 16, 16)
        for part in ac:
            begin(part)

        @pl.loop(0, ny // 4)
        def _(p):
            depth_adjoint(16 + 4 * p, 1)
            depth_adjoint(18 + 4 * p, 1)

        pick(sz, 16, ny, 0)
        begin(az)
        await_all(ac[0])
        add_depth(rc, 0, 0, 0, only, sides, "zd")
        give(0)
        await_all(ac[1])
        add_depth(rc, 1, only, rz_n - only, rz_n, sides, "zu")
        give(1)
        await_all(ac[2])
        add_depth(rc, 0, 0, only, rz_n, sides, "zd")
        add_depth(rc, 1, only, 0, rz_n - only, sides, "zu")
        give(2)
        await_all(az)
        add_depth(rz, 0, 0, 0, rz_n, whole, "zd")
        add_depth(rz, 1, only, 0, rz_n, whole, "zu")
        for part in ay:
            await_all(part)
        for n, y0, way in ((0, 16, "yd"), (1, ny, "yu")):
            @pl.when(has[way])
            def _():
                @pl.loop(0, nz)
                def _(i):
                    at = pl.ds((rz_n + i) * PITCH + y0, 16)
                    cor[at, :] = cor[at, :] + ry[n, i]

        @pl.loop(0, nz)
        def _(i):
            fresh = ext[rz_n + i] * cor[pl.ds((rz_n + i) * PITCH + 16, ny), :]
            ext[rz_n + i] = fresh
            out_ref[i] = fresh

        for n in range(3):
            drain(ac[n])
            drain(ay[n])
        drain(az)


def solution(mesh):
    n_gz, n_xy = mesh.shape["gz"], mesh.shape["xy"]

    def local(est, upright, turned, kd, kr, kc, offsets, block_views):
        nz, ny, nx = est.shape
        views, hz = kd.shape
        hy, hx = kr.shape[1], kc.shape[1]
        halfv = upright.shape[0]
        kk = views * nz
        stacked = -(-3 * kk // 128) * 128
        dma = pltpu.SemaphoreType.DMA
        vmem = pltpu.VMEM
        smem = pl.BlockSpec(memory_space=pltpu.SMEM)
        vspace = pl.BlockSpec(memory_space=pltpu.VMEM)
        anyspace = pl.BlockSpec(memory_space=pl.ANY)
        octets = halfv * (nz // 8)
        rz_n = (hz - 1) // 2
        return pl.pallas_call(
            functools.partial(kernel, nz, ny, views, halfv, n_gz, n_xy, hz, hy, hx),
            out_shape=jax.ShapeDtypeStruct((nz, ny, nx), F32),
            in_specs=[smem] + [vspace] * 4 + [anyspace] * 3,
            out_specs=vspace,
            scratch_shapes=[
                vmem((112, ny, 128), F32),
                vmem((112, 32, 128), F32),
                vmem((112 * PITCH, 128), F32),
                vmem(((kk + 16) * PITCH, 128), F32),
                vmem((112 * PITCH, 128), F32),
                vmem((2, rz_n, 32, 128), F32),
                vmem((2, rz_n, ny, 128), F32),
                vmem((2, nz, 16, 128), F32),
                vmem((2, rz_n, 32, 128), F32),
                vmem((2, rz_n, ny, 128), F32),
                vmem((2, nz, 16, 128), F32),
                vmem((views, nz, ny, 128), F32),
                vmem(turned.shape, F32),
                vmem((n_xy, octets, ny, 128), F32),
                vmem((n_xy, octets, ny, 128), F32),
                vmem((3, 8, 128), F32),
                vmem((stacked, 128), F32),
                vmem((112, stacked), F32),
                vmem((kk, 384), BF16),
                vmem((3, 112, stacked), BF16),
                vmem((views, ny, 256), BF16),
                vmem((views, 64, 128), BF16),
                vmem((views, 256, 256), BF16),
                vmem((views, 256, 256), BF16),
                vmem((16 * ny, 256), BF16),
                vmem((16 * ny, 256), BF16),
                vmem((8, 2 * ny, 256), BF16),
                dma((3,)),
                dma((2,)), dma((2,)), dma((6,)), dma((6,)), dma((4,)), dma((4,)),
                dma((2,)), dma((2,)), dma((4,)), dma((4,)), dma((6,)), dma((6,)),
                dma((n_xy - 1,)), dma((n_xy - 1,)),
            ],
            compiler_params=pltpu.CompilerParams(
                collective_id=0, has_side_effects=True, vmem_limit_bytes=60 * 1024 * 1024
            ),
            name="deconvolve",
        )(offsets.reshape(1, views), kd, kr, kc, block_views, est, upright, turned)

    in_specs = (
        P("gz", "xy", None),
        P(None, "gz", "xy", None),
        P(None, "gz", "xy", None),
        P(), P(), P(), P(), P(),
    )
    return jax.shard_map(
        local, mesh=mesh, in_specs=in_specs, out_specs=P("gz", "xy", None), check_vma=False
    )
```

```python
import functools

import jax
import jax.numpy as jnp
from jax import lax
from jax.experimental import pallas as pl
from jax.experimental.pallas import tpu as pltpu
from jax.sharding import PartitionSpec as P

ITERS = 2
PITCH = 66
F32 = jnp.float32
BF16 = jnp.bfloat16
MESH = pl.DeviceIdType.MESH


def split(value):
    high = value.astype(BF16)
    low = (value - high.astype(F32)).astype(BF16)
    return high, low


def row(shape):
    return lax.broadcasted_iota(jnp.int32, shape, 0)


def lane(shape):
    return lax.broadcasted_iota(jnp.int32, shape, 1)


def kernel(
    nz, ny, views, halfv, n_gz, n_xy, hz, hy, hx,
    off_ref, kd_ref, kr_ref, kc_ref, bv_ref, est_hbm, up_hbm, vt_hbm,
    out_ref,
    ext, rim, wide, mid, cor, sc, sz, sy, rc, rz, ry, obs, vt, pack, recv,
    taps, stack, flat, zl, zt, yf, ya, xf, xa, ahead, ratio, behind,
    load_sem, fz_send, fz_recv, fy_send, fy_recv, fc_send, fc_recv,
    az_send, az_recv, ac_send, ac_recv, ay_send, ay_recv, t_send, t_recv,
):
    g = lax.axis_index("gz")
    r = lax.axis_index("xy")
    rz_n = (hz - 1) // 2
    top = rz_n + nz
    kk = views * nz
    only = nz - rz_n
    spans = ((only, rz_n), (0, only), (rz_n, nz))
    has = {"zu": g < n_gz - 1, "zd": g > 0, "yu": r < n_xy - 1, "yd": r > 0}
    opposite = {"zu": "zd", "zd": "zu", "yu": "yd", "yd": "yu"}
    target = {"zu": {"gz": g + 1}, "zd": {"gz": g - 1}, "yu": {"xy": r + 1}, "yd": {"xy": r - 1}}

    loads = [
        pltpu.make_async_copy(est_hbm, ext.at[pl.ds(rz_n, nz)], load_sem.at[0]),
        pltpu.make_async_copy(vt_hbm, vt, load_sem.at[1]),
        pltpu.make_async_copy(up_hbm, obs.at[pl.ds(0, halfv)], load_sem.at[2]),
    ]
    for load in loads:
        load.start()

    barrier = pltpu.get_barrier_semaphore()
    for d in range(1, n_xy):
        pl.semaphore_signal(
            barrier, inc=1, device_id={"xy": lax.rem(r + d, n_xy)}, device_id_type=MESH
        )
    for way in ("zu", "zd"):
        @pl.when(has[way])
        def _():
            pl.semaphore_signal(barrier, inc=1, device_id=target[way], device_id_type=MESH)

    def clear(z0, z1, y0, y1, refs):
        @pl.loop(z0, z1)
        def _(i):
            for ref in refs:
                ref[i, pl.ds(y0, y1 - y0), :] = jnp.zeros((y1 - y0, 128), F32)

    clear(top + rz_n, ext.shape[0], 0, ny, (ext, rim))

    @pl.when(jnp.logical_not(has["zd"]))
    def _():
        clear(0, rz_n, 0, ny, (ext, rim))

    @pl.when(jnp.logical_not(has["zu"]))
    def _():
        clear(top, top + rz_n, 0, ny, (ext, rim))

    @pl.when(jnp.logical_not(has["yd"]))
    def _():
        clear(rz_n, top, 0, 16, (rim,))

    @pl.when(jnp.logical_not(has["yu"]))
    def _():
        clear(rz_n, top, 16, 32, (rim,))

    def flow(way, src, dst, send, recv_sem, number):
        def make():
            return pltpu.make_async_remote_copy(
                src_ref=src, dst_ref=dst, send_sem=send.at[number], recv_sem=recv_sem.at[number],
                device_id=target[way], device_id_type=MESH,
            )

        def start():
            @pl.when(has[way])
            def _():
                make().start()

        def arrived():
            @pl.when(has[opposite[way]])
            def _():
                make().wait_recv()

        def sent():
            @pl.when(has[way])
            def _():
                make().wait_send()

        return start, arrived, sent

    def rows(ref, z0, z1):
        return ref.at[pl.ds(z0, z1 - z0)]

    def cut(ref, z0, z1, y0):
        return ref.at[pl.ds(z0, z1 - z0), pl.ds(y0, 16), :]

    fz = [
        flow("zu", rows(ext, top - rz_n, top), rows(ext, 0, rz_n), fz_send, fz_recv, 0),
        flow("zd", rows(ext, rz_n, 2 * rz_n), rows(ext, top, top + rz_n), fz_send, fz_recv, 1),
    ]
    fy = []
    for n, (a, b) in enumerate(spans):
        a, b = rz_n + a, rz_n + b
        fy.append([
            flow("yu", cut(ext, a, b, ny - 16), cut(rim, a, b, 0), fy_send, fy_recv, 2 * n),
            flow("yd", cut(ext, a, b, 0), cut(rim, a, b, 16), fy_send, fy_recv, 2 * n + 1),
        ])
    fc = [
        [
            flow("zu", rows(rim, rz_n + only, 2 * rz_n), rows(rim, 0, rz_n - only), fc_send, fc_recv, 0),
            flow("zd", rows(rim, rz_n + only, 2 * rz_n), rows(rim, top + only, top + rz_n), fc_send, fc_recv, 1),
        ],
        [flow("zd", rows(rim, rz_n, rz_n + only), rows(rim, top, top + only), fc_send, fc_recv, 2)],
        [flow("zu", rows(rim, 2 * rz_n, top), rows(rim, rz_n - only, rz_n), fc_send, fc_recv, 3)],
    ]
    ac = [
        [flow("zu", rows(sc.at[0], 0, only), rows(rc.at[0], 0, only), ac_send, ac_recv, 0)],
        [flow("zd", rows(sc.at[1], rz_n - only, rz_n), rows(rc.at[1], rz_n - only, rz_n), ac_send, ac_recv, 1)],
        [
            flow("zu", rows(sc.at[0], only, rz_n), rows(rc.at[0], only, rz_n), ac_send, ac_recv, 2),
            flow("zd", rows(sc.at[1], 0, rz_n - only), rows(rc.at[1], 0, rz_n - only), ac_send, ac_recv, 3),
        ],
    ]
    az = [
        flow("zu", sz.at[0], rz.at[0], az_send, az_recv, 0),
        flow("zd", sz.at[1], rz.at[1], az_send, az_recv, 1),
    ]
    ay = []
    for n, (a, b) in enumerate((spans[1], spans[2], spans[0])):
        ay.append([
            flow("yu", rows(sy.at[0], a, b), rows(ry.at[0], a, b), ay_send, ay_recv, 2 * n),
            flow("yd", rows(sy.at[1], a, b), rows(ry.at[1], a, b), ay_send, ay_recv, 2 * n + 1),
        ])

    def begin(flows):
        for f in flows:
            f[0]()

    def await_all(flows):
        for f in flows:
            f[1]()

    def drain(flows):
        for f in flows:
            f[2]()

    loads[0].wait()
    greeted = n_xy - 1 + has["zu"].astype(jnp.int32) + has["zd"].astype(jnp.int32)
    pl.semaphore_wait(barrier, greeted)
    for part in fy:
        begin(part)
    begin(fz)

    loads[1].wait()
    octets = nz // 8

    @pl.loop(0, halfv * octets)
    def _(i):
        block = vt[i // octets, pl.ds((i % octets) * 8, 8)].reshape(128, ny * n_xy)
        for half in range(2):
            part = block[:, half * 128:(half + 1) * 128].T
            for piece in range(128 // ny):
                pack[half * (128 // ny) + piece, i] = part[piece * ny:(piece + 1) * ny]

    def turn(d):
        peer = lax.rem(r + d, n_xy)
        return pltpu.make_async_remote_copy(
            src_ref=pack.at[peer], dst_ref=recv.at[r], send_sem=t_send.at[d - 1], recv_sem=t_recv.at[d - 1],
            device_id={"xy": peer}, device_id_type=MESH,
        )

    for d in range(1, n_xy):
        turn(d).start()

    @pl.loop(0, halfv * octets)
    def _(i):
        recv[r, i] = pack[r, i]

    taps[...] = jnp.zeros_like(taps)
    for n, ref in enumerate((kd_ref, kr_ref, kc_ref)):
        value = ref[...]
        value = value / jnp.sum(value, axis=1, keepdims=True)
        taps[n, 0:views, 0:value.shape[1]] = value
        if n == 1:
            taps[n, 0:views, 64:64 + value.shape[1]] = value
    stack[...] = jnp.zeros_like(stack)

    @pl.loop(0, views)
    def _(v):
        def toeplitz(line, count, shift):
            return pltpu.roll(jnp.broadcast_to(line, (count, 128)), shift, 1, stride=1, stride_axis=0)

        depth = toeplitz(taps[0, pl.ds(v, 1), :], nz, 0)
        for n in range(3):
            stack[pl.ds(n * kk + v * nz, nz), :] = depth
        high, low = split(depth)
        zl[pl.ds(v * nz, nz), 0:128] = high
        zl[pl.ds(v * nz, nz), 128:256] = high
        zl[pl.ds(v * nz, nz), 256:384] = low

        line = toeplitz(taps[1, pl.ds(v, 1), :], ny, 1)
        high, low = split(line)
        yf[v, :, 0:128] = high
        yf[v, :, 128:256] = low
        line = jnp.concatenate([line] * (128 // ny), axis=0).T[0:64]
        high, low = split(line)
        ya[v] = jnp.where(lane((64, 128)) < 64, high.astype(F32), low.astype(F32)).astype(BF16)

        s = (128, 128)
        reach = (hx - 1) // 2
        shift = off_ref[0, v] + reach
        tap = lane(s) - row(s) + shift
        line = pltpu.roll(jnp.broadcast_to(taps[2, pl.ds(v, 1), :], (8, 128)), 128 - shift, 1)[0:1]
        column = jnp.where((tap >= 0) & (tap < hx), toeplitz(line, 128, 0), 0.0)
        for ref, matrix in ((xa, column), (xf, column.T)):
            high, low = split(matrix)
            ref[v, 0:128, 0:128] = high
            ref[v, 128:256, 0:128] = high
            ref[v, 0:128, 128:256] = low
            ref[v, 128:256, 128:256] = low

    for part in range(stack.shape[0] // 128):
        flat[:, part * 128:(part + 1) * 128] = stack[part * 128:(part + 1) * 128, :].T[0:112]

    for yb in range(3):
        fields = []
        for zb in range(3):
            block = jnp.clip(g + zb - 1, 0, n_gz - 1) * n_xy + jnp.clip(r + yb - 1, 0, n_xy - 1)
            held = lane(bv_ref.shape) == block
            chosen = jnp.sum(jnp.where(held, bv_ref[...], 0).astype(F32), axis=1, keepdims=True)
            view = (lax.rem(lane((1, stack.shape[0])), kk) // nz).astype(F32)
            field = jnp.zeros((1, stack.shape[0]), F32)
            for k in range(bv_ref.shape[0]):
                one = jnp.broadcast_to(chosen[k:k + 1, :], (1, stack.shape[0]))
                field = field + jnp.where(one == view, 1.0, 0.0)
            fields.append(field / float(bv_ref.shape[0]))

        for i in range(7):
            s = (16, stack.shape[0])
            number = row(s) + 16 * i
            field = jnp.where(number < rz_n, fields[0], jnp.where(number < top, fields[1], fields[2]))
            scaled = flat[16 * i:16 * i + 16, :] * field
            high, low = split(scaled)
            high, low = high.astype(F32), low.astype(F32)
            chosen = jnp.where(lane(s) < 2 * kk, high, low)
            zt[yb, 16 * i:16 * i + 16, :] = chosen.astype(BF16)

    def widen(source, z0, z1, y0, width, to):
        @pl.loop(z0, z1, unroll=6 if (z1 - z0) % 6 == 0 else 2)
        def _(i):
            wide[pl.ds(i * PITCH + to, width), :] = source[i, pl.ds(y0, width), :]

    def widen_rim(z0, z1):
        widen(rim, z0, z1, 0, 16, 0)
        widen(rim, z0, z1, 16, 16, 16 + ny)

    def depth_forward(y0):
        pair = jnp.concatenate(
            [wide[pl.ds(y0 + n, 112, stride=PITCH), :] for n in range(2)], axis=1
        )
        high, low = split(pair)
        gap = jnp.zeros((16, 256), BF16)
        first = jnp.concatenate([high, gap, low, gap], axis=0)
        second = jnp.concatenate([high, gap], axis=0)
        result = jnp.dot(zl[:, 0:256], first, preferred_element_type=F32)
        result = result + jnp.dot(zl[:, 256:384], second, preferred_element_type=F32)
        for n in range(2):
            mid[pl.ds(y0 + n, kk, stride=PITCH), :] = result[:, n * 128:(n + 1) * 128]

    def depth_adjoint(y0, yb):
        pair = jnp.concatenate(
            [mid[pl.ds(y0 + n, kk, stride=PITCH), :] for n in range(2)], axis=1
        )
        high, low = split(pair)
        gap = jnp.zeros((stack.shape[0] - 3 * kk, 256), BF16)
        operand = jnp.concatenate([high, low, high, gap], axis=0)
        result = jnp.dot(zt[yb], operand, preferred_element_type=F32)
        for n in range(2):
            cor[pl.ds(y0 + n, 112, stride=PITCH), :] = result[:, n * 128:(n + 1) * 128]

    group = 16
    groups = nz // group

    def middle(step):
        spare = views * nz
        count = views * groups

        @pl.loop(0, count + 3)
        def _(i):
            @pl.when((step == 0) & (i == halfv * groups))
            def _():
                unpack()

            def at(stage):
                number = jnp.clip(i - stage, 0, count - 1)
                return number // groups, (number % groups) * group

            v, z0 = at(3)
            base = jnp.where(i < 3, spare, v * nz + z0) * PITCH
            for p in range(group // 2):
                operand = jnp.concatenate([behind[p], behind[p, 0:ny]], axis=0)
                result = jnp.dot(ya[v, :, 0:96], operand, preferred_element_type=F32)
                mid[pl.ds(base + 2 * p * PITCH, 64), :] = result[:, 0:128]
                mid[pl.ds(base + (2 * p + 1) * PITCH, 64), :] = result[:, 128:256]

            v, z0 = at(2)
            both = jnp.dot(ratio[...], xa[v], preferred_element_type=F32)
            back = both[:, 0:128] + both[:, 128:256]
            for p in range(group // 2):
                pair = jnp.concatenate(
                    [back[(2 * p) * ny:(2 * p + 1) * ny], back[(2 * p + 1) * ny:(2 * p + 2) * ny]], axis=1
                )
                behind[p] = jnp.concatenate(split(pair), axis=0)

            v, z0 = at(1)
            both = jnp.dot(ahead[...], xf[v], preferred_element_type=F32)
            blurred = both[:, 0:128] + both[:, 128:256]
            quotient = obs[v, pl.ds(z0, group)].reshape(group * ny, 128) / blurred
            ratio[...] = jnp.concatenate(split(quotient), axis=1)

            v, z0 = at(0)
            base = (v * nz + z0) * PITCH
            for p in range(group // 2):
                pair = jnp.concatenate(
                    [mid[pl.ds(base + (2 * p + n) * PITCH, 64), :] for n in range(2)], axis=1
                )
                high, low = split(pair)
                result = jnp.dot(
                    yf[v, :, 0:192], jnp.concatenate([high, low, high], axis=0), preferred_element_type=F32
                )
                for n in range(2):
                    ahead[(2 * p + n) * ny:(2 * p + n + 1) * ny, :] = jnp.concatenate(
                        split(result[:, n * 128:(n + 1) * 128]), axis=1
                    )

    def unpack():
        for d in range(1, n_xy):
            turn(d).wait()
        per = 128 // n_xy

        @pl.loop(0, halfv * octets, unroll=2)
        def _(i):
            parts = [recv[j, i] for j in range(n_xy)]
            place = lane((ny, 128)) // per
            for d in (4, 2, 1):
                upper = (place & d) != 0
                for a in range(n_xy):
                    if a & d:
                        continue
                    first, second = parts[a], parts[a + d]
                    parts[a] = jnp.where(upper, pltpu.roll(second, per * d, 1), first)
                    parts[a + d] = jnp.where(upper, second, pltpu.roll(first, 128 - per * d, 1))
            for j in range(n_xy):
                obs[halfv + i // octets, (i % octets) * 8 + j] = parts[j]

    def add_depth(source, n, z0, i0, i1, pieces, way):
        @pl.when(has[way])
        def _():
            @pl.loop(i0, i1, unroll=6 if (i1 - i0) % 6 == 0 else 2)
            def _(i):
                for y0, width, to in pieces:
                    at = pl.ds((rz_n + z0 + i) * PITCH + to, width)
                    cor[at, :] = cor[at, :] + source[n, i, pl.ds(y0, width), :]

    sides = ((0, 16, 0), (16, 16, 16 + ny))
    whole = ((0, ny, 16),)

    def give(n):
        a, b = (spans[1], spans[2], spans[0])[n]

        @pl.loop(a, b, unroll=6)
        def _(i):
            sy[0, i] = cor[pl.ds((rz_n + i) * PITCH + 16 + ny, 16), :]
            sy[1, i] = cor[pl.ds((rz_n + i) * PITCH, 16), :]

        begin(ay[n])

    @pl.loop(0, ITERS)
    def _(step):
        @pl.when(step > 0)
        def _():
            for part in fy:
                begin(part)
            begin(fz)

        widen(ext, rz_n, top, 0, ny, 16)
        for n in range(3):
            await_all(fy[n])
            begin(fc[n])
        widen_rim(rz_n, top)
        await_all(fz)
        widen(ext, 0, rz_n, 0, ny, 16)
        widen(ext, top, ext.shape[0], 0, ny, 16)

        @pl.loop(0, ny // 8)
        def _(p):
            for n in range(4):
                depth_forward(16 + 8 * p + 2 * n)

        for n in range(3):
            await_all(fc[n])
        widen_rim(0, rz_n)
        widen_rim(top, ext.shape[0])

        @pl.loop(0, 4)
        def _(p):
            for n in range(2):
                depth_forward(4 * p + 2 * n)
                depth_forward(16 + ny + 4 * p + 2 * n)

        for n in range(3):
            drain(fy[n])
            drain(fc[n])
        drain(fz)

        @pl.when(step == 0)
        def _():
            loads[2].wait()

        middle(step)

        @pl.loop(0, 4)
        def _(p):
            for n in range(2):
                depth_adjoint(4 * p + 2 * n, 0)
                depth_adjoint(16 + ny + 4 * p + 2 * n, 2)

        def pick(dest, y0, width, to):
            @pl.loop(0, rz_n, unroll=6)
            def _(i):
                dest[0, i, pl.ds(to, width), :] = cor[pl.ds((top + i) * PITCH + y0, width), :]
                dest[1, i, pl.ds(to, width), :] = cor[pl.ds(i * PITCH + y0, width), :]

        pick(sc, 0, 16, 0)
        pick(sc, 16 + ny, 16, 16)
        for part in ac:
            begin(part)

        @pl.loop(0, ny // 8)
        def _(p):
            for n in range(4):
                depth_adjoint(16 + 8 * p + 2 * n, 1)

        pick(sz, 16, ny, 0)
        begin(az)
        await_all(ac[0])
        add_depth(rc, 0, 0, 0, only, sides, "zd")
        give(0)
        await_all(ac[1])
        add_depth(rc, 1, only, rz_n - only, rz_n, sides, "zu")
        give(1)
        await_all(ac[2])
        add_depth(rc, 0, 0, only, rz_n, sides, "zd")
        add_depth(rc, 1, only, 0, rz_n - only, sides, "zu")
        give(2)
        await_all(az)
        add_depth(rz, 0, 0, 0, rz_n, whole, "zd")
        add_depth(rz, 1, only, 0, rz_n, whole, "zu")
        for part in ay:
            await_all(part)
        for n, y0, way in ((0, 16, "yd"), (1, ny, "yu")):
            @pl.when(has[way])
            def _():
                @pl.loop(0, nz, unroll=6)
                def _(i):
                    at = pl.ds((rz_n + i) * PITCH + y0, 16)
                    cor[at, :] = cor[at, :] + ry[n, i]

        @pl.loop(0, nz, unroll=6)
        def _(i):
            fresh = ext[rz_n + i] * cor[pl.ds((rz_n + i) * PITCH + 16, ny), :]
            ext[rz_n + i] = fresh
            out_ref[i] = fresh

        for n in range(3):
            drain(ac[n])
            drain(ay[n])
        drain(az)


def solution(mesh):
    n_gz, n_xy = mesh.shape["gz"], mesh.shape["xy"]

    def local(est, upright, turned, kd, kr, kc, offsets, block_views):
        nz, ny, nx = est.shape
        views, hz = kd.shape
        hy, hx = kr.shape[1], kc.shape[1]
        halfv = upright.shape[0]
        kk = views * nz
        stacked = -(-3 * kk // 128) * 128
        dma = pltpu.SemaphoreType.DMA
        vmem = pltpu.VMEM
        smem = pl.BlockSpec(memory_space=pltpu.SMEM)
        vspace = pl.BlockSpec(memory_space=pltpu.VMEM)
        anyspace = pl.BlockSpec(memory_space=pl.ANY)
        octets = halfv * (nz // 8)
        rz_n = (hz - 1) // 2
        return pl.pallas_call(
            functools.partial(kernel, nz, ny, views, halfv, n_gz, n_xy, hz, hy, hx),
            out_shape=jax.ShapeDtypeStruct((nz, ny, nx), F32),
            in_specs=[smem] + [vspace] * 4 + [anyspace] * 3,
            out_specs=vspace,
            scratch_shapes=[
                vmem((112, ny, 128), F32),
                vmem((112, 32, 128), F32),
                vmem((112 * PITCH, 128), F32),
                vmem(((kk + 16) * PITCH, 128), F32),
                vmem((112 * PITCH, 128), F32),
                vmem((2, rz_n, 32, 128), F32),
                vmem((2, rz_n, ny, 128), F32),
                vmem((2, nz, 16, 128), F32),
                vmem((2, rz_n, 32, 128), F32),
                vmem((2, rz_n, ny, 128), F32),
                vmem((2, nz, 16, 128), F32),
                vmem((views, nz, ny, 128), F32),
                vmem(turned.shape, F32),
                vmem((n_xy, octets, ny, 128), F32),
                vmem((n_xy, octets, ny, 128), F32),
                vmem((3, 8, 128), F32),
                vmem((stacked, 128), F32),
                vmem((112, stacked), F32),
                vmem((kk, 384), BF16),
                vmem((3, 112, stacked), BF16),
                vmem((views, ny, 256), BF16),
                vmem((views, 64, 128), BF16),
                vmem((views, 256, 256), BF16),
                vmem((views, 256, 256), BF16),
                vmem((16 * ny, 256), BF16),
                vmem((16 * ny, 256), BF16),
                vmem((8, 2 * ny, 256), BF16),
                dma((3,)),
                dma((2,)), dma((2,)), dma((6,)), dma((6,)), dma((4,)), dma((4,)),
                dma((2,)), dma((2,)), dma((4,)), dma((4,)), dma((6,)), dma((6,)),
                dma((n_xy - 1,)), dma((n_xy - 1,)),
            ],
            compiler_params=pltpu.CompilerParams(
                collective_id=0, has_side_effects=True, vmem_limit_bytes=60 * 1024 * 1024
            ),
            name="deconvolve",
        )(offsets.reshape(1, views), kd, kr, kc, block_views.T, est, upright, turned)

    in_specs = (
        P("gz", "xy", None),
        P(None, "gz", "xy", None),
        P(None, "gz", "xy", None),
        P(), P(), P(), P(), P(),
    )
    return jax.shard_map(
        local, mesh=mesh, in_specs=in_specs, out_specs=P("gz", "xy", None), check_vma=False
    )
```

```python
import functools

import jax
import jax.numpy as jnp
from jax import lax
from jax.experimental import pallas as pl
from jax.experimental.pallas import tpu as pltpu
from jax.sharding import PartitionSpec as P

ITERS = 2
PITCH = 66
F32 = jnp.float32
BF16 = jnp.bfloat16
MESH = pl.DeviceIdType.MESH


def split(value):
    high = value.astype(BF16)
    low = (value - high.astype(F32)).astype(BF16)
    return high, low


def row(shape):
    return lax.broadcasted_iota(jnp.int32, shape, 0)


def lane(shape):
    return lax.broadcasted_iota(jnp.int32, shape, 1)


def kernel(
    nz, ny, views, halfv, n_gz, n_xy, hz, hy, hx,
    off_ref, kd_ref, kr_ref, kc_ref, bv_ref, est_hbm, up_hbm, vt_hbm,
    out_ref,
    ext, rim, wide, mid, cor, sc, sz, sy, rc, rz, ry, obs, vt, pack, recv,
    taps, stack, flat, zl, zt, yf, ya, xf, xa, ahead, ratio, behind,
    load_sem, fz_send, fz_recv, fy_send, fy_recv, fc_send, fc_recv,
    az_send, az_recv, ac_send, ac_recv, ay_send, ay_recv, t_send, t_recv,
):
    g = lax.axis_index("gz")
    r = lax.axis_index("xy")
    rz_n = (hz - 1) // 2
    top = rz_n + nz
    kk = views * nz
    only = nz - rz_n
    spans = ((only, rz_n), (0, only), (rz_n, nz))
    has = {"zu": g < n_gz - 1, "zd": g > 0, "yu": r < n_xy - 1, "yd": r > 0}
    opposite = {"zu": "zd", "zd": "zu", "yu": "yd", "yd": "yu"}
    target = {"zu": {"gz": g + 1}, "zd": {"gz": g - 1}, "yu": {"xy": r + 1}, "yd": {"xy": r - 1}}

    loads = [
        pltpu.make_async_copy(est_hbm, ext.at[pl.ds(rz_n, nz)], load_sem.at[0]),
        pltpu.make_async_copy(vt_hbm, vt, load_sem.at[1]),
        pltpu.make_async_copy(up_hbm, obs.at[pl.ds(0, halfv)], load_sem.at[2]),
    ]
    for load in loads:
        load.start()

    barrier = pltpu.get_barrier_semaphore()
    for d in range(1, n_xy):
        pl.semaphore_signal(
            barrier, inc=1, device_id={"xy": lax.rem(r + d, n_xy)}, device_id_type=MESH
        )
    for way in ("zu", "zd"):
        @pl.when(has[way])
        def _():
            pl.semaphore_signal(barrier, inc=1, device_id=target[way], device_id_type=MESH)

    def clear(z0, z1, y0, y1, refs):
        @pl.loop(z0, z1)
        def _(i):
            for ref in refs:
                ref[i, pl.ds(y0, y1 - y0), :] = jnp.zeros((y1 - y0, 128), F32)

    clear(top + rz_n, ext.shape[0], 0, ny, (ext, rim))

    @pl.when(jnp.logical_not(has["zd"]))
    def _():
        clear(0, rz_n, 0, ny, (ext, rim))

    @pl.when(jnp.logical_not(has["zu"]))
    def _():
        clear(top, top + rz_n, 0, ny, (ext, rim))

    @pl.when(jnp.logical_not(has["yd"]))
    def _():
        clear(rz_n, top, 0, 16, (rim,))

    @pl.when(jnp.logical_not(has["yu"]))
    def _():
        clear(rz_n, top, 16, 32, (rim,))

    def flow(way, src, dst, send, recv_sem, number):
        def make():
            return pltpu.make_async_remote_copy(
                src_ref=src, dst_ref=dst, send_sem=send.at[number], recv_sem=recv_sem.at[number],
                device_id=target[way], device_id_type=MESH,
            )

        def start():
            @pl.when(has[way])
            def _():
                make().start()

        def arrived():
            @pl.when(has[opposite[way]])
            def _():
                make().wait_recv()

        def sent():
            @pl.when(has[way])
            def _():
                make().wait_send()

        return start, arrived, sent

    def rows(ref, z0, z1):
        return ref.at[pl.ds(z0, z1 - z0)]

    def cut(ref, z0, z1, y0):
        return ref.at[pl.ds(z0, z1 - z0), pl.ds(y0, 16), :]

    fz = [
        flow("zu", rows(ext, top - rz_n, top), rows(ext, 0, rz_n), fz_send, fz_recv, 0),
        flow("zd", rows(ext, rz_n, 2 * rz_n), rows(ext, top, top + rz_n), fz_send, fz_recv, 1),
    ]
    fy = []
    for n, (a, b) in enumerate(spans):
        a, b = rz_n + a, rz_n + b
        fy.append([
            flow("yu", cut(ext, a, b, ny - 16), cut(rim, a, b, 0), fy_send, fy_recv, 2 * n),
            flow("yd", cut(ext, a, b, 0), cut(rim, a, b, 16), fy_send, fy_recv, 2 * n + 1),
        ])
    fc = [
        [
            flow("zu", rows(rim, rz_n + only, 2 * rz_n), rows(rim, 0, rz_n - only), fc_send, fc_recv, 0),
            flow("zd", rows(rim, rz_n + only, 2 * rz_n), rows(rim, top + only, top + rz_n), fc_send, fc_recv, 1),
        ],
        [flow("zd", rows(rim, rz_n, rz_n + only), rows(rim, top, top + only), fc_send, fc_recv, 2)],
        [flow("zu", rows(rim, 2 * rz_n, top), rows(rim, rz_n - only, rz_n), fc_send, fc_recv, 3)],
    ]
    ac = [
        [flow("zu", rows(sc.at[0], 0, only), rows(rc.at[0], 0, only), ac_send, ac_recv, 0)],
        [flow("zd", rows(sc.at[1], rz_n - only, rz_n), rows(rc.at[1], rz_n - only, rz_n), ac_send, ac_recv, 1)],
        [
            flow("zu", rows(sc.at[0], only, rz_n), rows(rc.at[0], only, rz_n), ac_send, ac_recv, 2),
            flow("zd", rows(sc.at[1], 0, rz_n - only), rows(rc.at[1], 0, rz_n - only), ac_send, ac_recv, 3),
        ],
    ]
    az = [
        flow("zu", sz.at[0], rz.at[0], az_send, az_recv, 0),
        flow("zd", sz.at[1], rz.at[1], az_send, az_recv, 1),
    ]
    ay = []
    for n, (a, b) in enumerate((spans[1], spans[2], spans[0])):
        ay.append([
            flow("yu", rows(sy.at[0], a, b), rows(ry.at[0], a, b), ay_send, ay_recv, 2 * n),
            flow("yd", rows(sy.at[1], a, b), rows(ry.at[1], a, b), ay_send, ay_recv, 2 * n + 1),
        ])

    def begin(flows):
        for f in flows:
            f[0]()

    def await_all(flows):
        for f in flows:
            f[1]()

    def drain(flows):
        for f in flows:
            f[2]()

    loads[0].wait()
    greeted = n_xy - 1 + has["zu"].astype(jnp.int32) + has["zd"].astype(jnp.int32)
    pl.semaphore_wait(barrier, greeted)
    for part in fy:
        begin(part)
    begin(fz)

    loads[1].wait()
    octets = nz // 8

    @pl.loop(0, halfv * octets, unroll=3)
    def _(i):
        block = vt[i // octets, pl.ds((i % octets) * 8, 8)].reshape(128, ny * n_xy)
        for half in range(2):
            part = block[:, half * 128:(half + 1) * 128].T
            for piece in range(128 // ny):
                pack[half * (128 // ny) + piece, i] = part[piece * ny:(piece + 1) * ny]

    def turn(d):
        peer = lax.rem(r + d, n_xy)
        return pltpu.make_async_remote_copy(
            src_ref=pack.at[peer], dst_ref=recv.at[r], send_sem=t_send.at[d - 1], recv_sem=t_recv.at[d - 1],
            device_id={"xy": peer}, device_id_type=MESH,
        )

    for d in range(1, n_xy):
        turn(d).start()

    @pl.loop(0, halfv * octets, unroll=3)
    def _(i):
        recv[r, i] = pack[r, i]

    taps[...] = jnp.zeros_like(taps)
    for n, ref in enumerate((kd_ref, kr_ref, kc_ref)):
        value = ref[...]
        value = value / jnp.sum(value, axis=1, keepdims=True)
        taps[n, 0:views, 0:value.shape[1]] = value
        if n == 1:
            taps[n, 0:views, 64:64 + value.shape[1]] = value
    stack[...] = jnp.zeros_like(stack)

    @pl.loop(0, views, unroll=2)
    def _(v):
        def toeplitz(line, count, shift):
            return pltpu.roll(jnp.broadcast_to(line, (count, 128)), shift, 1, stride=1, stride_axis=0)

        depth = toeplitz(taps[0, pl.ds(v, 1), :], nz, 0)
        for n in range(3):
            stack[pl.ds(n * kk + v * nz, nz), :] = depth
        high, low = split(depth)
        zl[pl.ds(v * nz, nz), 0:128] = high
        zl[pl.ds(v * nz, nz), 128:256] = high
        zl[pl.ds(v * nz, nz), 256:384] = low

        line = toeplitz(taps[1, pl.ds(v, 1), :], ny, 1)
        high, low = split(line)
        yf[v, :, 0:128] = high
        yf[v, :, 128:256] = low
        line = jnp.concatenate([line] * (128 // ny), axis=0).T[0:64]
        high, low = split(line)
        ya[v] = jnp.where(lane((64, 128)) < 64, high.astype(F32), low.astype(F32)).astype(BF16)

        s = (128, 128)
        reach = (hx - 1) // 2
        shift = off_ref[0, v] + reach
        tap = lane(s) - row(s) + shift
        line = pltpu.roll(jnp.broadcast_to(taps[2, pl.ds(v, 1), :], (8, 128)), 128 - shift, 1)[0:1]
        column = jnp.where((tap >= 0) & (tap < hx), toeplitz(line, 128, 0), 0.0)
        for ref, matrix in ((xa, column), (xf, column.T)):
            high, low = split(matrix)
            ref[v, 0:128, 0:128] = high
            ref[v, 128:256, 0:128] = high
            ref[v, 0:128, 128:256] = low
            ref[v, 128:256, 128:256] = low

    for part in range(stack.shape[0] // 128):
        flat[:, part * 128:(part + 1) * 128] = stack[part * 128:(part + 1) * 128, :].T[0:112]

    for yb in range(3):
        fields = []
        for zb in range(3):
            block = jnp.clip(g + zb - 1, 0, n_gz - 1) * n_xy + jnp.clip(r + yb - 1, 0, n_xy - 1)
            held = lane(bv_ref.shape) == block
            chosen = jnp.sum(jnp.where(held, bv_ref[...], 0).astype(F32), axis=1, keepdims=True)
            view = (lax.rem(lane((1, stack.shape[0])), kk) // nz).astype(F32)
            field = jnp.zeros((1, stack.shape[0]), F32)
            for k in range(bv_ref.shape[0]):
                one = jnp.broadcast_to(chosen[k:k + 1, :], (1, stack.shape[0]))
                field = field + jnp.where(one == view, 1.0, 0.0)
            fields.append(field / float(bv_ref.shape[0]))

        for i in range(7):
            s = (16, stack.shape[0])
            number = row(s) + 16 * i
            field = jnp.where(number < rz_n, fields[0], jnp.where(number < top, fields[1], fields[2]))
            scaled = flat[16 * i:16 * i + 16, :] * field
            high, low = split(scaled)
            high, low = high.astype(F32), low.astype(F32)
            chosen = jnp.where(lane(s) < 2 * kk, high, low)
            zt[yb, 16 * i:16 * i + 16, :] = chosen.astype(BF16)

    def widen(source, z0, z1, y0, width, to):
        @pl.loop(z0, z1, unroll=6 if (z1 - z0) % 6 == 0 else 2)
        def _(i):
            wide[pl.ds(i * PITCH + to, width), :] = source[i, pl.ds(y0, width), :]

    def widen_rim(z0, z1):
        widen(rim, z0, z1, 0, 16, 0)
        widen(rim, z0, z1, 16, 16, 16 + ny)

    def depth_forward(y0):
        pair = jnp.concatenate(
            [wide[pl.ds(y0 + n, 112, stride=PITCH), :] for n in range(2)], axis=1
        )
        high, low = split(pair)
        gap = jnp.zeros((16, 256), BF16)
        first = jnp.concatenate([high, gap, low, gap], axis=0)
        second = jnp.concatenate([high, gap], axis=0)
        result = jnp.dot(zl[:, 0:256], first, preferred_element_type=F32)
        result = result + jnp.dot(zl[:, 256:384], second, preferred_element_type=F32)
        for n in range(2):
            mid[pl.ds(y0 + n, kk, stride=PITCH), :] = result[:, n * 128:(n + 1) * 128]

    def depth_adjoint(y0, yb):
        pair = jnp.concatenate(
            [mid[pl.ds(y0 + n, kk, stride=PITCH), :] for n in range(2)], axis=1
        )
        high, low = split(pair)
        gap = jnp.zeros((stack.shape[0] - 3 * kk, 256), BF16)
        operand = jnp.concatenate([high, low, high, gap], axis=0)
        result = jnp.dot(zt[yb], operand, preferred_element_type=F32)
        for n in range(2):
            cor[pl.ds(y0 + n, 112, stride=PITCH), :] = result[:, n * 128:(n + 1) * 128]

    group = 16
    groups = nz // group

    def middle(step):
        spare = views * nz
        count = views * groups

        @pl.loop(0, count + 3)
        def _(i):
            @pl.when((step == 0) & (i == halfv * groups))
            def _():
                unpack()

            def at(stage):
                number = jnp.clip(i - stage, 0, count - 1)
                return number // groups, (number % groups) * group

            v, z0 = at(3)
            base = jnp.where(i < 3, spare, v * nz + z0) * PITCH
            for p in range(group // 2):
                operand = jnp.concatenate([behind[p], behind[p, 0:ny]], axis=0)
                result = jnp.dot(ya[v, :, 0:96], operand, preferred_element_type=F32)
                mid[pl.ds(base + 2 * p * PITCH, 64), :] = result[:, 0:128]
                mid[pl.ds(base + (2 * p + 1) * PITCH, 64), :] = result[:, 128:256]

            v, z0 = at(2)
            both = jnp.dot(ratio[...], xa[v], preferred_element_type=F32)
            back = both[:, 0:128] + both[:, 128:256]
            for p in range(group // 2):
                pair = jnp.concatenate(
                    [back[(2 * p) * ny:(2 * p + 1) * ny], back[(2 * p + 1) * ny:(2 * p + 2) * ny]], axis=1
                )
                behind[p] = jnp.concatenate(split(pair), axis=0)

            v, z0 = at(1)
            both = jnp.dot(ahead[...], xf[v], preferred_element_type=F32)
            blurred = both[:, 0:128] + both[:, 128:256]
            quotient = obs[v, pl.ds(z0, group)].reshape(group * ny, 128) / blurred
            ratio[...] = jnp.concatenate(split(quotient), axis=1)

            v, z0 = at(0)
            base = (v * nz + z0) * PITCH
            for p in range(group // 2):
                pair = jnp.concatenate(
                    [mid[pl.ds(base + (2 * p + n) * PITCH, 64), :] for n in range(2)], axis=1
                )
                high, low = split(pair)
                result = jnp.dot(
                    yf[v, :, 0:192], jnp.concatenate([high, low, high], axis=0), preferred_element_type=F32
                )
                for n in range(2):
                    ahead[(2 * p + n) * ny:(2 * p + n + 1) * ny, :] = jnp.concatenate(
                        split(result[:, n * 128:(n + 1) * 128]), axis=1
                    )

    def unpack():
        for d in range(1, n_xy):
            turn(d).wait()
        per = 128 // n_xy

        @pl.loop(0, halfv * octets, unroll=2)
        def _(i):
            parts = [recv[j, i] for j in range(n_xy)]
            place = lane((ny, 128)) // per
            for d in (4, 2, 1):
                upper = (place & d) != 0
                for a in range(n_xy):
                    if a & d:
                        continue
                    first, second = parts[a], parts[a + d]
                    parts[a] = jnp.where(upper, pltpu.roll(second, per * d, 1), first)
                    parts[a + d] = jnp.where(upper, second, pltpu.roll(first, 128 - per * d, 1))
            for j in range(n_xy):
                obs[halfv + i // octets, (i % octets) * 8 + j] = parts[j]

    def add_depth(source, n, z0, i0, i1, pieces, way):
        @pl.when(has[way])
        def _():
            @pl.loop(i0, i1, unroll=6 if (i1 - i0) % 6 == 0 else 2)
            def _(i):
                for y0, width, to in pieces:
                    at = pl.ds((rz_n + z0 + i) * PITCH + to, width)
                    cor[at, :] = cor[at, :] + source[n, i, pl.ds(y0, width), :]

    sides = ((0, 16, 0), (16, 16, 16 + ny))
    whole = ((0, ny, 16),)

    def give(n):
        a, b = (spans[1], spans[2], spans[0])[n]

        @pl.loop(a, b, unroll=6)
        def _(i):
            sy[0, i] = cor[pl.ds((rz_n + i) * PITCH + 16 + ny, 16), :]
            sy[1, i] = cor[pl.ds((rz_n + i) * PITCH, 16), :]

        begin(ay[n])

    @pl.loop(0, ITERS)
    def _(step):
        @pl.when(step > 0)
        def _():
            for part in fy:
                begin(part)
            begin(fz)

        widen(ext, rz_n, top, 0, ny, 16)
        for n in range(3):
            await_all(fy[n])
            begin(fc[n])
        widen_rim(rz_n, top)
        await_all(fz)
        widen(ext, 0, rz_n, 0, ny, 16)
        widen(ext, top, ext.shape[0], 0, ny, 16)

        @pl.loop(0, ny // 8)
        def _(p):
            for n in range(4):
                depth_forward(16 + 8 * p + 2 * n)

        for n in range(3):
            await_all(fc[n])
        widen_rim(0, rz_n)
        widen_rim(top, ext.shape[0])

        @pl.loop(0, 4)
        def _(p):
            for n in range(2):
                depth_forward(4 * p + 2 * n)
                depth_forward(16 + ny + 4 * p + 2 * n)

        for n in range(3):
            drain(fy[n])
            drain(fc[n])
        drain(fz)

        @pl.when(step == 0)
        def _():
            loads[2].wait()

        middle(step)

        @pl.loop(0, 4)
        def _(p):
            for n in range(2):
                depth_adjoint(4 * p + 2 * n, 0)
                depth_adjoint(16 + ny + 4 * p + 2 * n, 2)

        def pick(dest, y0, width, to):
            @pl.loop(0, rz_n, unroll=6)
            def _(i):
                dest[0, i, pl.ds(to, width), :] = cor[pl.ds((top + i) * PITCH + y0, width), :]
                dest[1, i, pl.ds(to, width), :] = cor[pl.ds(i * PITCH + y0, width), :]

        pick(sc, 0, 16, 0)
        pick(sc, 16 + ny, 16, 16)
        for part in ac:
            begin(part)

        @pl.loop(0, ny // 8)
        def _(p):
            for n in range(4):
                depth_adjoint(16 + 8 * p + 2 * n, 1)

        pick(sz, 16, ny, 0)
        begin(az)
        await_all(ac[0])
        add_depth(rc, 0, 0, 0, only, sides, "zd")
        give(0)
        await_all(ac[1])
        add_depth(rc, 1, only, rz_n - only, rz_n, sides, "zu")
        give(1)
        await_all(ac[2])
        add_depth(rc, 0, 0, only, rz_n, sides, "zd")
        add_depth(rc, 1, only, 0, rz_n - only, sides, "zu")
        give(2)
        await_all(az)
        add_depth(rz, 0, 0, 0, rz_n, whole, "zd")
        add_depth(rz, 1, only, 0, rz_n, whole, "zu")
        for part in ay:
            await_all(part)
        for n, y0, way in ((0, 16, "yd"), (1, ny, "yu")):
            @pl.when(has[way])
            def _():
                @pl.loop(0, nz, unroll=6)
                def _(i):
                    at = pl.ds((rz_n + i) * PITCH + y0, 16)
                    cor[at, :] = cor[at, :] + ry[n, i]

        @pl.loop(0, nz, unroll=6)
        def _(i):
            fresh = ext[rz_n + i] * cor[pl.ds((rz_n + i) * PITCH + 16, ny), :]
            ext[rz_n + i] = fresh
            out_ref[i] = fresh

        for n in range(3):
            drain(ac[n])
            drain(ay[n])
        drain(az)


def solution(mesh):
    n_gz, n_xy = mesh.shape["gz"], mesh.shape["xy"]

    def local(est, upright, turned, kd, kr, kc, offsets, block_views):
        nz, ny, nx = est.shape
        views, hz = kd.shape
        hy, hx = kr.shape[1], kc.shape[1]
        halfv = upright.shape[0]
        kk = views * nz
        stacked = -(-3 * kk // 128) * 128
        dma = pltpu.SemaphoreType.DMA
        vmem = pltpu.VMEM
        smem = pl.BlockSpec(memory_space=pltpu.SMEM)
        vspace = pl.BlockSpec(memory_space=pltpu.VMEM)
        anyspace = pl.BlockSpec(memory_space=pl.ANY)
        octets = halfv * (nz // 8)
        rz_n = (hz - 1) // 2
        return pl.pallas_call(
            functools.partial(kernel, nz, ny, views, halfv, n_gz, n_xy, hz, hy, hx),
            out_shape=jax.ShapeDtypeStruct((nz, ny, nx), F32),
            in_specs=[smem] + [vspace] * 4 + [anyspace] * 3,
            out_specs=vspace,
            scratch_shapes=[
                vmem((112, ny, 128), F32),
                vmem((112, 32, 128), F32),
                vmem((112 * PITCH, 128), F32),
                vmem(((kk + 16) * PITCH, 128), F32),
                vmem((112 * PITCH, 128), F32),
                vmem((2, rz_n, 32, 128), F32),
                vmem((2, rz_n, ny, 128), F32),
                vmem((2, nz, 16, 128), F32),
                vmem((2, rz_n, 32, 128), F32),
                vmem((2, rz_n, ny, 128), F32),
                vmem((2, nz, 16, 128), F32),
                vmem((views, nz, ny, 128), F32),
                vmem(turned.shape, F32),
                vmem((n_xy, octets, ny, 128), F32),
                vmem((n_xy, octets, ny, 128), F32),
                vmem((3, 8, 128), F32),
                vmem((stacked, 128), F32),
                vmem((112, stacked), F32),
                vmem((kk, 384), BF16),
                vmem((3, 112, stacked), BF16),
                vmem((views, ny, 256), BF16),
                vmem((views, 64, 128), BF16),
                vmem((views, 256, 256), BF16),
                vmem((views, 256, 256), BF16),
                vmem((16 * ny, 256), BF16),
                vmem((16 * ny, 256), BF16),
                vmem((8, 2 * ny, 256), BF16),
                dma((3,)),
                dma((2,)), dma((2,)), dma((6,)), dma((6,)), dma((4,)), dma((4,)),
                dma((2,)), dma((2,)), dma((4,)), dma((4,)), dma((6,)), dma((6,)),
                dma((n_xy - 1,)), dma((n_xy - 1,)),
            ],
            compiler_params=pltpu.CompilerParams(
                collective_id=0, has_side_effects=True, vmem_limit_bytes=60 * 1024 * 1024
            ),
            name="deconvolve",
        )(offsets.reshape(1, views), kd, kr, kc, block_views.T, est, upright, turned)

    in_specs = (
        P("gz", "xy", None),
        P(None, "gz", "xy", None),
        P(None, "gz", "xy", None),
        P(), P(), P(), P(), P(),
    )
    return jax.shard_map(
        local, mesh=mesh, in_specs=in_specs, out_specs=P("gz", "xy", None), check_vma=False
    )
```
